512 devices in a mesh: pole: 4 (over z_lo, core), row: 8 (over y), col: 16 (over x, z_hi).
Axes of the slice: x: 4, y: 8, z: 8 (z_hi: 4, z_lo: 2; z = z_hi * 2 + z_lo), core: 2. Of those that a mesh axis runs over, the one named last changes fastest.
Arguments:
- inverse: bfloat16 [12, 2, 6144, 6144], P('pole', None, 'col', 'row'), may hold values from -0.078125 to 0.078125
- lower: bfloat16 [12, 2, 6144, 512], P('pole', None, 'row', 'col'), may hold values from -6 to 6
- mask_tiles: int32 [16, 16], replicated, may hold values from 0 to 1, as said below
- pole_weight: float32 [12, 2], P('pole'), may hold values from -4 to 4
Outputs:
- panel: bfloat16 [12, 2, 6144, 512], P('pole', None, 'col', 'row')
- density: float32 [6144, 512], P(('col', 'pole'), 'row')
The draws below stay inside these ranges and needn't reach their ends.
Inputs may be any that keep to these rules, and one draw needn't show every extreme that they name: `mask_tiles`: each tile row is either all ones or holds exactly one 1; of tile rows t and t + 8 exactly one is all ones.
All inputs are finite; a program needn't handle non-finite values.
Results may differ from the reference program's by a relative error of at most 0.017.
Values may be sent and summed in bfloat16 or wider, within the bound.
A program may use at most 128 MiB of HBM per device.

```python
import jax
import jax.numpy as jnp
from jax import lax

TILE = 384
NT = 16
PANEL = 512
ORDER = 6144
POLES = 12
N_ROW = 8


def draw_mask_tiles(key, part):
    first_key = jax.random.fold_in(key, 11)
    second_key = jax.random.fold_in(key, 23)
    half_rows = NT // 2
    heavy_low = jax.random.randint(first_key, (half_rows,), 0, 2)
    single_col = jax.random.randint(second_key, (NT,), 0, NT)
    tile_rows = jnp.arange(NT, dtype=jnp.int32)
    tile_cols = jnp.arange(NT, dtype=jnp.int32)
    paired = heavy_low[tile_rows % half_rows]
    heavy = jnp.where(tile_rows < half_rows, paired == 1, paired == 0)
    single = (tile_cols[None, :] == single_col[:, None]).astype(jnp.int32)
    return jnp.where(heavy[:, None], jnp.ones((NT, NT), jnp.int32), single).astype(jnp.int32)


def strengthened(entries, rng, source, target, shards_of, factor):
    def block_of(axis_at):
        return (jnp.arange(entries.shape[axis_at]) // (entries.shape[axis_at] // shards_of)).reshape((-1,) + (1,) * (entries.ndim - 1 - axis_at))

    near = jax.random.permutation(rng, shards_of)[block_of(target)]
    second = (block_of(target) + shards_of // 2) % shards_of
    return jnp.where((block_of(source) == near) | (block_of(source) == second), factor * entries, entries)


def block_scale(stream_key, dims, pieces, least, largest):
    loudness, own = 1.0, jax.random.fold_in(stream_key, 6)
    for axis_at, blocks in pieces:
        heights = jnp.exp(jax.random.uniform(jax.random.fold_in(own, axis_at), (blocks,), jnp.float32, least / len(pieces), largest / len(pieces)))
        loudness = loudness * jnp.repeat(heights, dims[axis_at] // blocks).reshape([-1 if axis == axis_at else 1 for axis in range(len(dims))])
    return loudness


def normal_values(stream_key, shape, deviation, bound, pieces=(), held_as=jnp.bfloat16):
    array = jax.random.normal(stream_key, shape, jnp.float32) * deviation
    if len(pieces) > 0:
        array = block_scale(stream_key, shape, pieces, -0.22, 0.18) * array
    return jnp.clip(array, min=-bound, max=bound).astype(held_as)


def heavy_noise(own_key, dims, deviation, limit, cuts, heavy, kind=jnp.bfloat16):
    array = deviation * jax.random.normal(own_key, dims, jnp.float32)
    if cuts:
        array = array * block_scale(own_key, dims, cuts, -0.22, 0.18)
    return jnp.clip(strengthened(array, jax.random.fold_in(own_key, 3), *heavy), -limit, limit).astype(kind)


def setup_inputs(seed: int = 0) -> dict:
    streams_of = jax.random.split(jax.random.key(seed), 5)
    inverse = normal_values(streams_of[0], (POLES, 2, ORDER, ORDER), ORDER ** -0.5, 0.078125, ((0, 4), (2, 16), (3, 8)))
    lower = heavy_noise(streams_of[1], (POLES, 2, ORDER, PANEL), 1.0, 6.0, ((0, 4), (2, 8), (3, 16)), (2, 3, 16, 2.0))
    mask_tiles = draw_mask_tiles(jax.random.fold_in(streams_of[4], 71), 0)
    pole_weight = normal_values(streams_of[3], (POLES, 2), 1.0, 4.0, ((0, 4),), jnp.float32)
    return dict(inverse=inverse, lower=lower, mask_tiles=mask_tiles, pole_weight=pole_weight)


def reference(inverse, lower, mask_tiles, pole_weight):
    keep = jnp.repeat(jnp.repeat(mask_tiles, TILE, axis=0), TILE, axis=1).astype(jnp.bfloat16)
    width = ORDER // N_ROW
    panels = []
    for pole_idx in range(POLES):
        kept = inverse[pole_idx] * keep[None]
        total = jnp.zeros((2, ORDER, PANEL), jnp.float32)
        for block in range(N_ROW):
            lo_col = block * width
            a_re = kept[0, :, lo_col:lo_col + width]
            a_im = kept[1, :, lo_col:lo_col + width]
            l_re = lower[pole_idx, 0, lo_col:lo_col + width]
            l_im = lower[pole_idx, 1, lo_col:lo_col + width]
            real_part = jnp.dot(a_re, l_re, preferred_element_type=jnp.float32) - jnp.dot(a_im, l_im, preferred_element_type=jnp.float32)
            imag_part = jnp.dot(a_re, l_im, preferred_element_type=jnp.float32) + jnp.dot(a_im, l_re, preferred_element_type=jnp.float32)
            rounded = lax.optimization_barrier(jnp.stack([real_part, imag_part]).astype(jnp.bfloat16))
            total = total + rounded.astype(jnp.float32)
        panels.append((-total).astype(jnp.bfloat16))
    panel = jnp.stack(panels)
    values = panel.astype(jnp.float32)
    density = jnp.sum(pole_weight[:, 0, None, None] * values[:, 1] + pole_weight[:, 1, None, None] * values[:, 0], axis=0)
    return panel, density
```

```python
import functools

import jax
import jax.numpy as jnp
from jax import lax
from jax.experimental import pallas as pl
from jax.experimental.pallas import tpu as pltpu
from jax.sharding import PartitionSpec as P

MESH = pl.DeviceIdType.MESH
NX = 4
NZ = 4
NY = 8
NP = 4
KP = 3
TILE = 384
DEPTH = 768
WIDE = 32
OWN = 64
FULL = 512
PIECE = 96

ALL, LOW, HIGH = (0, 32), (0, 16), (16, 16)
TRANSFERS = (
    ((0, 0), ("z", 1), (0, -1), ALL),
    ((0, 0), ("z", -1), (0, 1), ALL),
    ((0, 0), ("x", 1), (-1, 0), ALL),
    ((0, 0), ("x", -1), (1, 0), ALL),
    ((0, -1), ("z", 1), (0, 2), LOW),
    ((0, 1), ("z", -1), (0, 2), HIGH),
    ((0, -1), ("x", 1), (-1, -1), ALL),
    ((0, -1), ("x", -1), (1, -1), ALL),
    ((0, 1), ("x", 1), (-1, 1), ALL),
    ((0, 1), ("x", -1), (1, 1), ALL),
    ((0, 2), ("x", 1), (-1, 2), ALL),
    ((0, 2), ("x", -1), (1, 2), ALL),
    ((-1, 0), ("x", 1), (2, 0), ALL),
    ((1, 2), ("x", -1), (2, 2), ALL),
    ((2, 0), ("z", 1), (2, -1), ALL),
    ((2, 0), ("z", -1), (2, 1), ALL),
)
NT = len(TRANSFERS)
NS = 7
NSUB = 2


def plan():
    steps = []
    for k in range(KP):
        steps += [("send", k, j) for j in (0, 1, 2, 3)]
    steps += [("own", 0, 0), ("weights", 0, 0)]
    for k in range(KP):
        ag = [
            [("get", k, 0)] + [("send", k, j) for j in (4, 6, 7)],
            [("get", k, 1)] + [("send", k, j) for j in (5, 8, 9)],
            [("get", k, 2), ("send", k, 12)],
            [("get", k, 4), ("get", k, 5)] + [("send", k, j) for j in (10, 11)],
            [("get", k, 12)] + [("send", k, j) for j in (14, 15)],
            [("get", k, 11), ("send", k, 13)],
            [("get", k, j) for j in (3, 6, 7, 8, 9, 10, 13, 14, 15)],
        ]
        rs = [[("reduce", k - 1, s)] for s in (1, 2, 3)] if k else []
        for i, group in enumerate(ag):
            steps += group
            if rs and i in (1, 3, 5):
                steps += rs.pop(0)
        if k:
            steps += [("finish", k - 1, 0)]
        steps += [("multiply", k, 0), ("reduce", k, 0)]
        if k + 1 < KP:
            steps += [("own", k + 1, 0), ("weights", k + 1, 0)]
    steps += [("reduce", KP - 1, s) for s in (1, 2, 3)]
    steps += [("finish", KP - 1, 0)]
    return steps


def kernel(
    inverse_ref, lower_ref, mask_ref, weight_ref, panel_ref, density_ref,
    block, factor, gathered, product, outgoing, incoming, pieces, pieces_out, pieces_in,
    block_sem, send_sem, recv_sem, rsend_sem, rrecv_sem, psend_sem, precv_sem,
):
    pole = lax.axis_index("pole")
    row = lax.axis_index("row")
    col = lax.axis_index("col")
    x, z = col // NZ, col % NZ

    def place(dx, dz):
        return lax.rem(x + NX + dx, NX) * NZ + lax.rem(z + NZ + dz, NZ)

    def along(step):
        axis, by = step
        return place(by, 0) if axis == "x" else place(0, by)

    def row_at(by):
        return lax.rem(row + NY + by, NY)

    def pole_at(by):
        return lax.rem(pole + by, NP)

    loads = [
        pltpu.make_async_copy(inverse_ref.at[k], block.at[k], block_sem.at[k]) for k in range(KP)
    ]
    for load in loads:
        load.start()

    barrier = pltpu.get_barrier_semaphore()
    for step in (("x", 1), ("x", -1), ("z", 1), ("z", -1)):
        pl.semaphore_signal(barrier, inc=1, device_id={"col": along(step)}, device_id_type=MESH)
    for by in (1, -1):
        pl.semaphore_signal(barrier, inc=1, device_id={"row": row_at(by)}, device_id_type=MESH)
    for by in (1, 2, 3):
        pl.semaphore_signal(barrier, inc=1, device_id={"pole": pole_at(by)}, device_id_type=MESH)
    pl.semaphore_wait(barrier, 9)

    def spot(k, chunk, rows):
        first = pl.multiple_of(place(*chunk) * WIDE + rows[0], 16)
        return gathered.at[k, :, pl.ds(first, rows[1]), :]

    def transfer(k, j, receiving):
        sent, step, got, rows = TRANSFERS[j]
        where = spot(k, got if receiving else sent, rows)
        source = where
        if not receiving and sent == (0, 0):
            source = lower_ref.at[k]
        return pltpu.make_async_remote_copy(
            src_ref=source,
            dst_ref=where,
            send_sem=send_sem.at[k, j],
            recv_sem=recv_sem.at[k, j],
            device_id={"col": along(step)},
            device_id_type=MESH,
        )

    def send(k, j):
        transfer(k, j, False).start()

    def get(k, j):
        transfer(k, j, True).wait_recv()

    def own(k, _):
        first = pl.multiple_of(place(0, 0) * WIDE, WIDE)
        gathered[k, :, pl.ds(first, WIDE), :] = lower_ref[k]

    def weights(k, _):
        loads[k].wait()
        left = mask_ref[col, 2 * row].astype(jnp.float32)
        right = mask_ref[col, 2 * row + 1].astype(jnp.float32)
        lane = lax.broadcasted_iota(jnp.int32, (1, DEPTH), 1)
        keep = jnp.where(lane < TILE, left, right)

        def some(i, carry):
            first = pl.multiple_of(i * 64, 64)
            re = block[k, 0, pl.ds(first, 64), :].astype(jnp.float32) * keep
            im = block[k, 1, pl.ds(first, 64), :].astype(jnp.float32) * keep
            minus_re = (-re).astype(jnp.bfloat16)
            factor[k, 0, pl.ds(first, 64), :DEPTH] = minus_re
            factor[k, 0, pl.ds(first, 64), DEPTH:] = im.astype(jnp.bfloat16)
            factor[k, 1, pl.ds(first, 64), :DEPTH] = (-im).astype(jnp.bfloat16)
            factor[k, 1, pl.ds(first, 64), DEPTH:] = minus_re
            return carry

        lax.fori_loop(0, TILE // 64, some, 0)

    def multiply(k, _):
        def some(i, carry):
            first = pl.multiple_of(i * 256, 256)
            both = jnp.concatenate(
                [gathered[k, 0, pl.ds(first, 256), :], gathered[k, 1, pl.ds(first, 256), :]], axis=1
            )
            for part in range(2):
                product[k, part, pl.ds(first, 256), :] = lax.dot_general(
                    both, factor[k, part], (((1,), (1,)), ((), ())), preferred_element_type=jnp.float32
                )
            return carry

        lax.fori_loop(0, FULL // 256, some, 0)

    def chains(k):
        turn = 1 if k % 2 == 0 else -1
        return ((0, turn, 4), (4, -turn, 3))

    def hop(k, slot, sub, to):
        return pltpu.make_async_remote_copy(
            src_ref=outgoing.at[k, slot, sub],
            dst_ref=incoming.at[k, slot, sub],
            send_sem=rsend_sem.at[k, slot, sub],
            recv_sem=rrecv_sem.at[k, slot, sub],
            device_id={"row": row_at(to)},
            device_id_type=MESH,
        )

    def mine(k, sub, owner):
        return product[k, sub, pl.ds(pl.multiple_of(owner * OWN, OWN), OWN), :]

    def reduce(k, s):
        for sub in range(NSUB):
            for base, turn, hops in chains(k):
                if s >= hops:
                    continue
                value = mine(k, sub, row_at(turn * (hops - s)))
                if s:
                    hop(k, base + s - 1, sub, turn).wait_recv()
                    value = value + incoming[k, base + s - 1, sub].astype(jnp.float32)
                outgoing[k, base + s, sub] = value.astype(jnp.bfloat16)
                hop(k, base + s, sub, turn).start()

    def finish(k, _):
        for sub in range(NSUB):
            value = mine(k, sub, row)
            for base, turn, hops in chains(k):
                hop(k, base + hops - 1, sub, turn).wait_recv()
                value = value + incoming[k, base + hops - 1, sub].astype(jnp.float32)
            panel_ref[k, sub] = value.astype(jnp.bfloat16)

    doing = dict(
        send=send, get=get, own=own, weights=weights, multiply=multiply, reduce=reduce, finish=finish
    )
    for what, k, index in plan():
        doing[what](k, index)

    weighted = jnp.zeros((OWN, TILE), jnp.float32)
    for k in range(KP):
        weighted = weighted + weight_ref[0, k] * panel_ref[k, 1].astype(jnp.float32)
        weighted = weighted + weight_ref[1, k] * panel_ref[k, 0].astype(jnp.float32)
    for q in range(NP):
        piece = weighted if q == 0 else pltpu.roll(weighted, TILE - PIECE * q, 1)
        pieces[q] = piece[:, :128]
        pieces_out[q] = piece[:, :128].astype(jnp.bfloat16)
    exchange = [
        pltpu.make_async_remote_copy(
            src_ref=pieces_out.at[pole_at(by)],
            dst_ref=pieces_in.at[by - 1],
            send_sem=psend_sem.at[by - 1],
            recv_sem=precv_sem.at[by - 1],
            device_id={"pole": pole_at(by)},
            device_id_type=MESH,
        )
        for by in range(1, NP)
    ]
    for copy in exchange:
        copy.start()
    total = pieces[pole]
    for by in range(1, NP):
        exchange[by - 1].wait_recv()
        total = total + pieces_in[by - 1].astype(jnp.float32)
    density_ref[...] = total[:, :PIECE]

    for copy in exchange:
        copy.wait_send()
    for k in range(KP):
        for j in range(NT):
            transfer(k, j, False).wait_send()
        for base, turn, hops in chains(k):
            for s in range(hops):
                for sub in range(NSUB):
                    hop(k, base + s, sub, turn).wait_send()


def body(inverse, lower, mask_tiles, pole_weight):
    vmem = pl.BlockSpec(memory_space=pltpu.VMEM)
    smem = pl.BlockSpec(memory_space=pltpu.SMEM)
    bf16, f32 = jnp.bfloat16, jnp.float32
    panel, density = pl.pallas_call(
        kernel,
        out_shape=(
            jax.ShapeDtypeStruct((KP, 2, OWN, TILE), bf16),
            jax.ShapeDtypeStruct((OWN, PIECE), f32),
        ),
        in_specs=[pl.BlockSpec(memory_space=pl.ANY), vmem, smem, smem],
        out_specs=(vmem, vmem),
        scratch_shapes=[
            pltpu.VMEM((KP, 2, TILE, DEPTH), bf16),
            pltpu.VMEM((KP, 2, TILE, 2 * DEPTH), bf16),
            pltpu.VMEM((KP, 2, FULL, DEPTH), bf16),
            pltpu.VMEM((KP, 2, FULL, TILE), f32),
            pltpu.VMEM((KP, NS, NSUB, OWN, TILE), bf16),
            pltpu.VMEM((KP, NS, NSUB, OWN, TILE), bf16),
            pltpu.VMEM((NP, OWN, 128), f32),
            pltpu.VMEM((NP, OWN, 128), bf16),
            pltpu.VMEM((NP - 1, OWN, 128), bf16),
            pltpu.SemaphoreType.DMA((KP,)),
            pltpu.SemaphoreType.DMA((KP, NT)),
            pltpu.SemaphoreType.DMA((KP, NT)),
            pltpu.SemaphoreType.DMA((KP, NS, NSUB)),
            pltpu.SemaphoreType.DMA((KP, NS, NSUB)),
            pltpu.SemaphoreType.DMA((NP - 1,)),
            pltpu.SemaphoreType.DMA((NP - 1,)),
        ],
        compiler_params=pltpu.CompilerParams(
            collective_id=0, has_side_effects=True, vmem_limit_bytes=56 * 1024 * 1024
        ),
        name="panel_update",
    )(inverse, jnp.swapaxes(lower, 2, 3), mask_tiles, jnp.swapaxes(pole_weight, 0, 1))
    return jnp.swapaxes(panel, 2, 3), jnp.swapaxes(density, 0, 1)


def solution(mesh):
    return jax.shard_map(
        body,
        mesh=mesh,
        in_specs=(
            P("pole", None, "col", "row"),
            P("pole", None, "row", "col"),
            P(),
            P("pole", None),
        ),
        out_specs=(P("pole", None, "col", "row"), P(("col", "pole"), "row")),
        check_vma=False,
    )
```

```python
import jax
import jax.numpy as jnp
from jax import lax
from jax.experimental import pallas as pl
from jax.experimental.pallas import tpu as pltpu
from jax.sharding import PartitionSpec as P

MESH = pl.DeviceIdType.MESH
NX = 4
NZ = 4
NY = 8
NP = 4
KP = 3
TILE = 384
DEPTH = 768
WIDE = 32
OWN = 64
FULL = 512
PIECE = 96

ALL, LOW, HIGH = (0, 32), (0, 16), (16, 16)
TRANSFERS = (
    ((0, 0), ("z", 1), (0, -1), ALL),
    ((0, 0), ("z", -1), (0, 1), ALL),
    ((0, 0), ("x", 1), (-1, 0), ALL),
    ((0, 0), ("x", -1), (1, 0), ALL),
    ((0, -1), ("z", 1), (0, 2), LOW),
    ((0, 1), ("z", -1), (0, 2), HIGH),
    ((0, -1), ("x", 1), (-1, -1), ALL),
    ((0, -1), ("x", -1), (1, -1), ALL),
    ((0, 1), ("x", 1), (-1, 1), ALL),
    ((0, 1), ("x", -1), (1, 1), ALL),
    ((0, 2), ("x", 1), (-1, 2), ALL),
    ((0, 2), ("x", -1), (1, 2), ALL),
    ((-1, 0), ("x", 1), (2, 0), ALL),
    ((1, 2), ("x", -1), (2, 2), ALL),
    ((2, 0), ("z", 1), (2, -1), ALL),
    ((2, 0), ("z", -1), (2, 1), ALL),
)
NT = len(TRANSFERS)
NS = 7
SUBS = (2, 2, 4)
TILES = (2, 2, 4)

STEPS = (
    (0, 1, 2), (0, 0, 2), (0, 3, 3), (0, 0, 1), (0, 0, 0), (0, 0, 3), (0, 1, 1), (0, 5, 2), (0, 1, 0), (0, 1, 3),
    (1, 1, 2), (0, 2, 2), (0, 3, 2), (0, 1, 12), (0, 2, 1), (0, 4, 3), (0, 3, 0), (0, 2, 3), (0, 5, 3), (2, 0, 0),
    (1, 3, 3), (1, 0, 2), (0, 0, 12), (0, 3, 1), (0, 2, 0), (1, 0, 3), (1, 0, 1), (0, 0, 9), (1, 0, 0), (1, 5, 2),
    (0, 0, 6), (0, 0, 7), (1, 1, 3), (1, 2, 2), (0, 0, 8), (0, 0, 5), (0, 0, 4), (1, 4, 3), (1, 1, 1), (0, 1, 9),
    (1, 1, 0), (1, 3, 2), (0, 1, 6), (0, 1, 5), (0, 1, 4), (0, 1, 7), (1, 2, 3), (1, 1, 12), (0, 1, 8), (0, 1, 15),
    (0, 1, 14), (1, 5, 3), (1, 2, 1), (0, 2, 9), (1, 3, 0), (1, 0, 12), (0, 2, 8), (0, 3, 7), (1, 0, 9), (1, 0, 6),
    (0, 3, 6), (0, 0, 15), (0, 3, 4), (1, 0, 7), (1, 3, 1), (0, 3, 9), (1, 2, 0), (1, 0, 8), (0, 2, 6), (0, 2, 7),
    (0, 2, 4), (1, 1, 9), (1, 0, 5), (1, 0, 4), (1, 1, 6), (0, 0, 10), (0, 2, 5), (0, 0, 11), (0, 0, 14), (1, 1, 7),
    (1, 1, 5), (1, 1, 4), (1, 1, 8), (0, 1, 10), (0, 1, 11), (0, 3, 5), (1, 2, 9), (1, 2, 8), (0, 3, 12), (0, 4, 1),
    (0, 4, 0), (1, 3, 7), (1, 1, 15), (1, 1, 14), (1, 3, 6), (0, 4, 2), (1, 3, 9), (1, 3, 4), (1, 2, 6), (0, 2, 12),
    (0, 5, 1), (0, 5, 0), (1, 2, 7), (1, 0, 15), (1, 2, 4), (1, 0, 10), (0, 3, 8), (1, 0, 11), (0, 0, 13),
    (1, 2, 5), (0, 2, 11), (1, 1, 10), (0, 2, 10), (1, 1, 11), (0, 1, 13), (1, 3, 5), (0, 3, 11), (1, 0, 14),
    (1, 3, 12), (0, 3, 15), (0, 3, 10), (0, 3, 14), (1, 0, 13), (1, 4, 2), (0, 4, 12), (1, 2, 11), (0, 2, 13),
    (1, 4, 1), (0, 4, 5), (0, 4, 9), (1, 4, 0), (0, 4, 4), (0, 4, 7), (1, 2, 12), (0, 4, 6), (0, 2, 15), (0, 2, 14),
    (1, 1, 13), (0, 4, 8), (0, 5, 12), (3, 0, 0), (4, 0, 0), (4, 0, 32), (4, 0, 1), (4, 0, 33), (3, 0, 1),
    (2, 1, 0), (1, 3, 8), (1, 3, 11), (0, 3, 13), (1, 5, 1), (0, 5, 8), (0, 5, 5), (0, 5, 9), (1, 5, 0), (0, 5, 4),
    (0, 5, 6), (0, 5, 7), (1, 2, 10), (1, 2, 13), (1, 3, 10), (1, 4, 9), (1, 3, 15), (1, 3, 14), (1, 4, 12),
    (0, 4, 14), (0, 4, 15), (4, 0, 8), (4, 0, 40), (1, 4, 7), (1, 4, 5), (1, 4, 4), (0, 4, 11), (1, 4, 6),
    (0, 4, 10), (4, 0, 9), (4, 0, 41), (1, 4, 8), (1, 3, 13), (1, 2, 15), (1, 2, 14), (3, 1, 0), (4, 0, 16),
    (4, 0, 48), (4, 1, 0), (4, 1, 32), (4, 1, 1), (4, 0, 17), (4, 0, 49), (4, 1, 33), (3, 1, 1), (2, 2, 0),
    (1, 5, 12), (0, 5, 15), (0, 5, 14), (1, 5, 9), (1, 5, 5), (1, 5, 4), (0, 5, 10), (0, 5, 11), (1, 5, 8),
    (1, 5, 7), (1, 5, 6), (1, 4, 11), (0, 4, 13), (1, 4, 15), (1, 4, 14), (1, 4, 10), (4, 0, 24), (4, 1, 40),
    (4, 1, 8), (4, 0, 25), (4, 1, 9), (1, 5, 10), (1, 5, 11), (0, 5, 13), (4, 1, 41), (1, 4, 13), (5, 0, 0),
    (4, 1, 16), (1, 5, 15), (1, 5, 14), (4, 1, 48), (4, 1, 17), (1, 5, 13), (3, 2, 0), (4, 2, 0), (4, 2, 32),
    (4, 2, 1), (4, 2, 33), (4, 2, 2), (4, 2, 34), (4, 2, 3), (4, 2, 35), (4, 1, 24), (4, 1, 49), (5, 0, 1),
    (3, 2, 1), (4, 1, 25), (3, 2, 2), (4, 2, 8), (4, 2, 40), (4, 2, 9), (4, 2, 41), (4, 2, 10), (4, 2, 42),
    (3, 2, 3), (4, 2, 11), (4, 2, 43), (5, 1, 0), (4, 2, 16), (5, 1, 1), (4, 2, 17), (4, 2, 48), (4, 2, 18),
    (4, 2, 49), (4, 2, 19), (4, 2, 50), (4, 2, 24), (4, 2, 51), (4, 2, 25), (4, 2, 26), (4, 2, 27), (5, 2, 0),
    (5, 2, 1), (5, 2, 2), (5, 2, 3),
)


def kernel(
    inverse_ref, lower_ref, mask_ref, weight_ref, panel_ref, density_ref,
    block, factor, gathered, product, outgoing, incoming, panel, pieces, pieces_out, pieces_in,
    block_sem, own_sem, panel_sem, send_sem, recv_sem, rsend_sem, rrecv_sem, psend_sem, precv_sem,
):
    pole = lax.axis_index("pole")
    row = lax.axis_index("row")
    col = lax.axis_index("col")
    x, z = col // NZ, col % NZ

    def place(dx, dz):
        return lax.rem(x + NX + dx, NX) * NZ + lax.rem(z + NZ + dz, NZ)

    def along(step):
        axis, by = step
        return place(by, 0) if axis == "x" else place(0, by)

    def row_at(by):
        return lax.rem(row + NY + by, NY)

    def pole_at(by):
        return lax.rem(pole + by, NP)

    loads = [
        pltpu.make_async_copy(inverse_ref.at[k], block.at[k], block_sem.at[k]) for k in range(KP)
    ]
    first_own = pl.multiple_of(place(0, 0) * WIDE, WIDE)
    own = pltpu.make_async_copy(lower_ref, gathered.at[:, :, pl.ds(first_own, WIDE), :], own_sem)
    own.start()
    for load in loads:
        load.start()

    barrier = pltpu.get_barrier_semaphore()
    for step in (("x", 1), ("x", -1), ("z", 1), ("z", -1)):
        pl.semaphore_signal(barrier, inc=1, device_id={"col": along(step)}, device_id_type=MESH)
    for by in (1, -1):
        pl.semaphore_signal(barrier, inc=1, device_id={"row": row_at(by)}, device_id_type=MESH)
    for by in (1, 2, 3):
        pl.semaphore_signal(barrier, inc=1, device_id={"pole": pole_at(by)}, device_id_type=MESH)
    pl.semaphore_wait(barrier, 9)

    def spot(slab, chunk, rows):
        first = pl.multiple_of(place(*chunk) * WIDE + rows[0], 16)
        return gathered.at[slab // 2, slab % 2, pl.ds(first, rows[1]), :]

    def transfer(slab, j, receiving):
        sent, step, got, rows = TRANSFERS[j]
        where = spot(slab, got if receiving else sent, rows)
        source = where
        if not receiving and sent == (0, 0):
            source = lower_ref.at[slab // 2, slab % 2]
        return pltpu.make_async_remote_copy(
            src_ref=source,
            dst_ref=where,
            send_sem=send_sem.at[slab, j],
            recv_sem=recv_sem.at[slab, j],
            device_id={"col": along(step)},
            device_id_type=MESH,
        )

    def send(slab, j):
        transfer(slab, j, False).start()

    def get(slab, j):
        transfer(slab, j, True).wait_recv()

    def weights(k, _):
        loads[k].wait()
        if k == 0:
            own.wait()
        left = mask_ref[col, 2 * row].astype(jnp.float32)
        right = mask_ref[col, 2 * row + 1].astype(jnp.float32)
        lane = lax.broadcasted_iota(jnp.int32, (1, DEPTH), 1)
        keep = jnp.where(lane < TILE, left, right)

        def some(i, carry):
            first = pl.multiple_of(i * 64, 64)
            re = block[k, 0, pl.ds(first, 64), :].astype(jnp.float32) * keep
            im = block[k, 1, pl.ds(first, 64), :].astype(jnp.float32) * keep
            minus_re = (-re).astype(jnp.bfloat16)
            factor[k, 0, pl.ds(first, 64), :DEPTH] = minus_re
            factor[k, 0, pl.ds(first, 64), DEPTH:] = im.astype(jnp.bfloat16)
            factor[k, 1, pl.ds(first, 64), :DEPTH] = (-im).astype(jnp.bfloat16)
            factor[k, 1, pl.ds(first, 64), DEPTH:] = minus_re
            return carry

        lax.fori_loop(0, TILE // 64, some, 0)

    def turn_of(k):
        return 1 if k % 2 == 0 else -1

    def multiply(k, tile):
        turn = turn_of(k)
        places = range(tile * 4 // TILES[k], (tile + 1) * 4 // TILES[k])
        blocks = [(q, side) for q in places for side in range(2)]
        lines = []
        for q, side in blocks:
            owner = row_at(turn * (4 - q)) if side == 0 else row_at(-turn * (3 - q))
            rows = pl.ds(pl.multiple_of(owner * OWN, OWN), OWN)
            lines.append(jnp.concatenate([gathered[k, 0, rows, :], gathered[k, 1, rows, :]], axis=1))
        both = jnp.concatenate(lines, axis=0)
        for part in range(2):
            value = lax.dot_general(
                both, factor[k, part], (((1,), (1,)), ((), ())), preferred_element_type=jnp.float32
            )
            for i, (q, side) in enumerate(blocks):
                product[k, part, q, side] = value[i * OWN : (i + 1) * OWN]

    def part_of(k, sub):
        each = 2 * OWN // SUBS[k]
        per = SUBS[k] // 2
        return sub // per, pl.ds(sub % per * each, each)

    def hop_copy(k, slot, sub):
        part, rows = part_of(k, sub)
        to = turn_of(k) if slot < 4 else -turn_of(k)
        return pltpu.make_async_remote_copy(
            src_ref=outgoing.at[k, slot, part, rows, :],
            dst_ref=incoming.at[k, slot, part, rows, :],
            send_sem=rsend_sem.at[k, slot, sub],
            recv_sem=rrecv_sem.at[k, slot, sub],
            device_id={"row": row_at(to)},
            device_id_type=MESH,
        )

    def hop(k, index):
        slot, sub = index // 8, index % 8
        part, rows = part_of(k, sub)
        q, side = (slot, 0) if slot < 4 else (slot - 4, 1)
        value = product[k, part, q, side, rows, :]
        if q:
            hop_copy(k, slot - 1, sub).wait_recv()
            value = value + incoming[k, slot - 1, part, rows, :].astype(jnp.float32)
        outgoing[k, slot, part, rows, :] = value.astype(jnp.bfloat16)
        hop_copy(k, slot, sub).start()

    def finish(k, sub):
        part, rows = part_of(k, sub)
        value = product[k, part, 3, 1, rows, :]
        for slot in (3, 6):
            hop_copy(k, slot, sub).wait_recv()
            value = value + incoming[k, slot, part, rows, :].astype(jnp.float32)
        panel[k, part, rows, :] = value.astype(jnp.bfloat16)

    stores = [
        pltpu.make_async_copy(panel.at[k], panel_ref.at[k], panel_sem.at[k]) for k in range(KP)
    ]
    doing = (send, get, weights, multiply, hop, finish)
    left = list(SUBS)
    for what, k, index in STEPS:
        doing[what](k, index)
        if what == 5:
            left[k] -= 1
            if left[k] == 0:
                stores[k].start()

    weighted = jnp.zeros((OWN, TILE), jnp.float32)
    for k in range(KP):
        weighted = weighted + weight_ref[0, k] * panel[k, 1].astype(jnp.float32)
        weighted = weighted + weight_ref[1, k] * panel[k, 0].astype(jnp.float32)
    for q in range(NP):
        piece = weighted if q == 0 else pltpu.roll(weighted, TILE - PIECE * q, 1)
        pieces[q] = piece[:, :128]
        pieces_out[q] = piece[:, :128].astype(jnp.bfloat16)
    exchange = [
        pltpu.make_async_remote_copy(
            src_ref=pieces_out.at[pole_at(by)],
            dst_ref=pieces_in.at[by - 1],
            send_sem=psend_sem.at[by - 1],
            recv_sem=precv_sem.at[by - 1],
            device_id={"pole": pole_at(by)},
            device_id_type=MESH,
        )
        for by in range(1, NP)
    ]
    for copy in exchange:
        copy.start()

    for slab in range(2 * KP):
        for j in range(NT):
            transfer(slab, j, False).wait_send()
    for k in range(KP):
        stores[k].wait()
        for slot in range(NS):
            for sub in range(SUBS[k]):
                hop_copy(k, slot, sub).wait_send()

    total = pieces[pole]
    for copy in exchange:
        copy.wait()
    for by in range(1, NP):
        total = total + pieces_in[by - 1].astype(jnp.float32)
    density_ref[...] = total[:, :PIECE]


def body(inverse, lower, mask_tiles, pole_weight):
    anywhere = pl.BlockSpec(memory_space=pl.ANY)
    vmem = pl.BlockSpec(memory_space=pltpu.VMEM)
    smem = pl.BlockSpec(memory_space=pltpu.SMEM)
    bf16, f32 = jnp.bfloat16, jnp.float32
    panel, density = pl.pallas_call(
        kernel,
        out_shape=(
            jax.ShapeDtypeStruct((KP, 2, OWN, TILE), bf16),
            jax.ShapeDtypeStruct((OWN, PIECE), f32),
        ),
        in_specs=[anywhere, anywhere, smem, smem],
        out_specs=(anywhere, vmem),
        scratch_shapes=[
            pltpu.VMEM((KP, 2, TILE, DEPTH), bf16),
            pltpu.VMEM((KP, 2, TILE, 2 * DEPTH), bf16),
            pltpu.VMEM((KP, 2, FULL, DEPTH), bf16),
            pltpu.VMEM((KP, 2, 4, 2, OWN, TILE), f32),
            pltpu.VMEM((KP, NS, 2, OWN, TILE), bf16),
            pltpu.VMEM((KP, NS, 2, OWN, TILE), bf16),
            pltpu.VMEM((KP, 2, OWN, TILE), bf16),
            pltpu.VMEM((NP, OWN, 128), f32),
            pltpu.VMEM((NP, OWN, 128), bf16),
            pltpu.VMEM((NP - 1, OWN, 128), bf16),
            pltpu.SemaphoreType.DMA((KP,)),
            pltpu.SemaphoreType.DMA,
            pltpu.SemaphoreType.DMA((KP,)),
            pltpu.SemaphoreType.DMA((2 * KP, NT)),
            pltpu.SemaphoreType.DMA((2 * KP, NT)),
            pltpu.SemaphoreType.DMA((KP, NS, max(SUBS))),
            pltpu.SemaphoreType.DMA((KP, NS, max(SUBS))),
            pltpu.SemaphoreType.DMA((NP - 1,)),
            pltpu.SemaphoreType.DMA((NP - 1,)),
        ],
        compiler_params=pltpu.CompilerParams(
            collective_id=0, has_side_effects=True, vmem_limit_bytes=56 * 1024 * 1024
        ),
        name="panel_update",
    )(inverse, jnp.swapaxes(lower, 2, 3), mask_tiles, jnp.swapaxes(pole_weight, 0, 1))
    return jnp.swapaxes(panel, 2, 3), jnp.swapaxes(density, 0, 1)


def solution(mesh):
    return jax.shard_map(
        body,
        mesh=mesh,
        in_specs=(
            P("pole", None, "col", "row"),
            P("pole", None, "row", "col"),
            P(),
            P("pole", None),
        ),
        out_specs=(P("pole", None, "col", "row"), P(("col", "pole"), "row")),
        check_vma=False,
    )
```

```python
import jax
import jax.numpy as jnp
from jax import lax
from jax.experimental import pallas as pl
from jax.experimental.pallas import tpu as pltpu
from jax.sharding import PartitionSpec as P

MESH = pl.DeviceIdType.MESH
NX = 4
NZ = 4
NY = 8
NP = 4
KP = 3
TILE = 384
DEPTH = 768
WIDE = 32
OWN = 64
FULL = 512
PIECE = 96

ALL, LOW, HIGH = (0, 32), (0, 16), (16, 16)
TRANSFERS = (
    ((0, 0), ("z", 1), (0, -1), ALL),
    ((0, 0), ("z", -1), (0, 1), ALL),
    ((0, 0), ("x", 1), (-1, 0), ALL),
    ((0, 0), ("x", -1), (1, 0), ALL),
    ((0, -1), ("z", 1), (0, 2), LOW),
    ((0, 1), ("z", -1), (0, 2), HIGH),
    ((0, -1), ("x", 1), (-1, -1), ALL),
    ((0, -1), ("x", -1), (1, -1), ALL),
    ((0, 1), ("x", 1), (-1, 1), ALL),
    ((0, 1), ("x", -1), (1, 1), ALL),
    ((0, 2), ("x", 1), (-1, 2), ALL),
    ((0, 2), ("x", -1), (1, 2), ALL),
    ((-1, 0), ("x", 1), (2, 0), ALL),
    ((1, 2), ("x", -1), (2, 2), ALL),
    ((2, 0), ("z", 1), (2, -1), ALL),
    ((2, 0), ("z", -1), (2, 1), ALL),
)
NT = len(TRANSFERS)
NU = 2 * KP
HALF = OWN // 2
NS = 7
SUBS = (1, 1, 1, 1, 1, 2)

CHAIN = ((4, 1, ()), (3, 1, (0,)), (2, 1, (1,)), (1, 1, (2,)), (-3, -1, ()), (-2, -1, (4,)), (-1, -1, (5,)))
FAN = ((4, 2, ()), (3, 1, ()), (-3, -1, ()), (1, 1, ()), (-1, -1, ()), (2, 2, (0, 1)), (-2, -2, (2,)))
CHAIN_ENDS, FAN_ENDS = (3, 6), (3, 4, 5, 6)
LAST = NU - 1
OWNERS = ((4, 3, -3, 2, -2, 1, -1, 0),) * LAST + ((4, 3, -3, 1, -1, 2, -2, 0),)
TILES = (1, 1, 1, 1, 1, 2)

STEPS = (
    (0, 0, 2), (0, 0, 0), (0, 0, 1), (0, 1, 2), (0, 1, 1), (0, 2, 2), (0, 3, 3), (0, 0, 3), (0, 2, 3), (0, 1, 0),
    (1, 0, 2), (0, 0, 12), (0, 2, 1), (0, 3, 2), (0, 4, 3), (0, 5, 2), (0, 1, 3), (0, 3, 0), (0, 5, 3), (2, 0, 0),
    (0, 3, 1), (0, 2, 0), (1, 3, 3), (1, 1, 2), (0, 1, 12), (1, 0, 3), (1, 0, 0), (0, 0, 7), (1, 0, 1), (1, 2, 2),
    (0, 0, 6), (1, 2, 3), (0, 0, 9), (1, 0, 12), (0, 0, 5), (0, 0, 4), (0, 0, 15), (0, 0, 8), (0, 0, 14), (1, 4, 3),
    (1, 1, 0), (0, 1, 7), (1, 1, 1), (1, 3, 2), (0, 1, 8), (0, 1, 9), (1, 1, 3), (1, 5, 2), (0, 2, 12), (0, 1, 4),
    (0, 1, 5), (1, 5, 3), (1, 3, 0), (0, 3, 7), (1, 2, 1), (1, 1, 12), (0, 2, 9), (0, 1, 14), (0, 2, 5), (0, 2, 8),
    (1, 0, 7), (1, 0, 6), (0, 1, 6), (1, 0, 9), (0, 1, 15), (1, 2, 0), (0, 2, 7), (1, 3, 1), (1, 0, 8), (0, 3, 8),
    (0, 2, 4), (0, 3, 9), (1, 1, 7), (1, 0, 4), (1, 0, 5), (1, 1, 8), (0, 0, 10), (0, 3, 4), (0, 3, 5), (0, 0, 11),
    (1, 1, 9), (1, 2, 12), (0, 3, 6), (0, 2, 14), (0, 2, 15), (1, 3, 7), (1, 0, 14), (1, 0, 15), (1, 2, 8),
    (0, 3, 12), (1, 2, 9), (1, 1, 4), (1, 1, 5), (0, 1, 11), (1, 1, 6), (0, 1, 10), (0, 5, 0), (0, 5, 1), (1, 2, 7),
    (1, 2, 5), (1, 3, 8), (0, 4, 2), (1, 3, 9), (1, 1, 14), (1, 0, 10), (0, 5, 12), (0, 4, 0), (0, 4, 1),
    (1, 0, 11), (0, 0, 13), (1, 2, 4), (0, 2, 11), (1, 1, 15), (3, 0, 0), (0, 2, 10), (4, 0, 0), (4, 0, 32),
    (0, 2, 6), (1, 3, 6), (1, 1, 11), (0, 1, 13), (1, 3, 4), (1, 3, 5), (0, 3, 11), (1, 3, 12), (1, 1, 10),
    (0, 3, 15), (0, 3, 14), (0, 3, 10), (1, 2, 14), (1, 2, 15), (1, 0, 13), (1, 4, 2), (0, 4, 12), (1, 2, 11),
    (0, 2, 13), (4, 0, 8), (4, 0, 40), (1, 5, 12), (0, 5, 15), (0, 5, 14), (1, 5, 0), (0, 5, 7), (0, 5, 6),
    (1, 5, 1), (0, 5, 9), (1, 1, 13), (0, 5, 8), (3, 1, 0), (0, 5, 4), (0, 5, 5), (4, 1, 0), (4, 1, 32), (2, 1, 0),
    (1, 2, 10), (1, 3, 11), (0, 3, 13), (1, 2, 6), (1, 4, 0), (0, 4, 4), (0, 4, 6), (0, 4, 7), (1, 4, 1), (0, 4, 5),
    (0, 4, 8), (0, 4, 9), (1, 3, 10), (1, 2, 13), (4, 0, 16), (4, 0, 48), (1, 4, 12), (0, 4, 14), (0, 4, 15),
    (1, 5, 7), (1, 3, 14), (1, 3, 15), (3, 2, 0), (4, 2, 0), (4, 1, 8), (4, 1, 40), (4, 2, 32), (1, 5, 6),
    (1, 5, 9), (1, 5, 8), (1, 3, 13), (3, 3, 0), (4, 0, 24), (4, 3, 0), (4, 3, 32), (2, 2, 0), (1, 5, 14),
    (1, 5, 15), (1, 4, 6), (1, 4, 7), (1, 5, 4), (1, 5, 5), (0, 5, 11), (0, 5, 10), (1, 4, 8), (1, 4, 9), (1, 4, 4),
    (1, 4, 5), (0, 4, 11), (0, 4, 10), (4, 2, 8), (4, 1, 16), (4, 1, 48), (4, 2, 40), (1, 4, 14), (1, 4, 15),
    (3, 4, 0), (4, 3, 8), (4, 4, 0), (4, 4, 32), (5, 0, 0), (1, 5, 11), (0, 5, 13), (1, 5, 10), (4, 3, 40),
    (1, 4, 11), (0, 4, 13), (4, 1, 24), (1, 4, 10), (4, 2, 16), (4, 2, 48), (4, 3, 16), (4, 4, 8), (1, 5, 13),
    (4, 4, 40), (4, 3, 48), (1, 4, 13), (3, 5, 0), (4, 2, 24), (4, 5, 0), (4, 5, 1), (4, 5, 8), (4, 5, 9),
    (4, 5, 16), (4, 5, 17), (5, 1, 0), (3, 5, 1), (4, 4, 16), (4, 3, 24), (4, 5, 24), (4, 5, 25), (4, 5, 32),
    (4, 5, 33), (4, 4, 48), (5, 2, 0), (4, 5, 41), (4, 5, 48), (4, 5, 40), (4, 5, 49), (5, 3, 0), (4, 4, 24),
    (5, 5, 1), (5, 5, 0), (5, 4, 0),
)


def kernel(
    inverse_ref, lower_ref, mask_ref, weight_ref, panel_ref, density_ref,
    block, factor, gathered, product, outgoing, incoming, panel, pieces, pieces_out, pieces_in,
    block_sem, own_sem, panel_sem, send_sem, recv_sem, rsend_sem, rrecv_sem, psend_sem, precv_sem,
):
    pole = lax.axis_index("pole")
    row = lax.axis_index("row")
    col = lax.axis_index("col")
    x, z = col // NZ, col % NZ

    def place(dx, dz):
        return lax.rem(x + NX + dx, NX) * NZ + lax.rem(z + NZ + dz, NZ)

    def along(step):
        axis, by = step
        return place(by, 0) if axis == "x" else place(0, by)

    def row_at(by):
        return lax.rem(row + NY + by, NY)

    def pole_at(by):
        return lax.rem(pole + by, NP)

    loads = [
        pltpu.make_async_copy(inverse_ref.at[k], block.at[k], block_sem.at[k]) for k in range(KP)
    ]
    first_own = pl.multiple_of(place(0, 0) * WIDE, WIDE)
    own = pltpu.make_async_copy(lower_ref, gathered.at[:, :, pl.ds(first_own, WIDE), :], own_sem)
    own.start()
    for load in loads:
        load.start()

    barrier = pltpu.get_barrier_semaphore()
    for step in (("x", 1), ("x", -1), ("z", 1), ("z", -1)):
        pl.semaphore_signal(barrier, inc=1, device_id={"col": along(step)}, device_id_type=MESH)
    for by in (1, -1, 2, -2):
        pl.semaphore_signal(barrier, inc=1, device_id={"row": row_at(by)}, device_id_type=MESH)
    for by in (1, 2, 3):
        pl.semaphore_signal(barrier, inc=1, device_id={"pole": pole_at(by)}, device_id_type=MESH)
    pl.semaphore_wait(barrier, 11)

    def spot(slab, chunk, rows):
        first = pl.multiple_of(place(*chunk) * WIDE + rows[0], 16)
        return gathered.at[slab // 2, slab % 2, pl.ds(first, rows[1]), :]

    def transfer(slab, j, receiving):
        sent, step, got, rows = TRANSFERS[j]
        where = spot(slab, got if receiving else sent, rows)
        source = where
        if not receiving and sent == (0, 0):
            source = lower_ref.at[slab // 2, slab % 2]
        return pltpu.make_async_remote_copy(
            src_ref=source,
            dst_ref=where,
            send_sem=send_sem.at[slab, j],
            recv_sem=recv_sem.at[slab, j],
            device_id={"col": along(step)},
            device_id_type=MESH,
        )

    def send(slab, j):
        transfer(slab, j, False).start()

    def get(slab, j):
        transfer(slab, j, True).wait_recv()

    def weights(k, _):
        loads[k].wait()
        if k == 0:
            own.wait()
        left = mask_ref[col, 2 * row].astype(jnp.float32)
        right = mask_ref[col, 2 * row + 1].astype(jnp.float32)
        lane = lax.broadcasted_iota(jnp.int32, (1, DEPTH), 1)
        keep = jnp.where(lane < TILE, left, right)

        def some(i, carry):
            first = pl.multiple_of(i * 64, 64)
            re = block[k, 0, pl.ds(first, 64), :].astype(jnp.float32) * keep
            im = block[k, 1, pl.ds(first, 64), :].astype(jnp.float32) * keep
            minus_re = (-re).astype(jnp.bfloat16)
            factor[k, 0, pl.ds(first, 64), :DEPTH] = minus_re
            factor[k, 0, pl.ds(first, 64), DEPTH:] = im.astype(jnp.bfloat16)
            factor[k, 1, pl.ds(first, 64), :DEPTH] = (-im).astype(jnp.bfloat16)
            factor[k, 1, pl.ds(first, 64), DEPTH:] = minus_re
            return carry

        lax.fori_loop(0, TILE // 64, some, 0)

    def spread(unit, owner):
        odd = lax.rem(z + 1 + unit % 2, 2)
        return pl.ds(pl.multiple_of(row_at(owner) * OWN + odd * HALF, HALF), HALF)

    def multiply(unit, tile):
        k = unit // 2
        each = 8 // TILES[unit]
        owners = OWNERS[unit][tile * each : (tile + 1) * each]
        lines = []
        for owner in owners:
            rows = spread(unit, owner)
            lines.append(jnp.concatenate([gathered[k, 0, rows, :], gathered[k, 1, rows, :]], axis=1))
        both = jnp.concatenate(lines, axis=0)
        for part in range(2):
            value = lax.dot_general(
                both, factor[k, part], (((1,), (1,)), ((), ())), preferred_element_type=jnp.float32
            )
            for i, owner in enumerate(owners):
                product[unit, part, owner % 8] = value[i * HALF : (i + 1) * HALF]

    def way(unit, slot, sub):
        turn = 1 if (sub if unit == LAST else unit) % 2 == 0 else -1
        owner, step, needs = (FAN if unit == LAST else CHAIN)[slot]
        return turn * owner % 8, turn * step, needs

    def parts_of(unit, sub):
        return slice(None) if SUBS[unit] == 1 else slice(sub, sub + 1)

    def hop_copy(unit, slot, sub):
        parts = pl.ds(0, 2) if SUBS[unit] == 1 else pl.ds(sub, 1)
        return pltpu.make_async_remote_copy(
            src_ref=outgoing.at[unit, slot, parts],
            dst_ref=incoming.at[unit, slot, parts],
            send_sem=rsend_sem.at[unit, slot, sub],
            recv_sem=rrecv_sem.at[unit, slot, sub],
            device_id={"row": row_at(way(unit, slot, sub)[1])},
            device_id_type=MESH,
        )

    def summed(unit, owner, slots, sub):
        parts = parts_of(unit, sub)
        value = product[unit, parts, owner]
        for slot in slots:
            hop_copy(unit, slot, sub).wait_recv()
            value = value + incoming[unit, slot, parts].astype(jnp.float32)
        return value.astype(jnp.bfloat16)

    def hop(unit, index):
        slot, sub = index // 8, index % 8
        owner, _, needs = way(unit, slot, sub)
        outgoing[unit, slot, parts_of(unit, sub)] = summed(unit, owner, needs, sub)
        hop_copy(unit, slot, sub).start()

    def finish(unit, sub):
        odd = lax.rem(z + 1 + unit % 2, 2)
        rows = pl.ds(pl.multiple_of(odd * HALF, HALF), HALF)
        ends = FAN_ENDS if unit == LAST else CHAIN_ENDS
        panel[unit // 2, parts_of(unit, sub), rows, :] = summed(unit, 0, ends, sub)

    stores = [
        pltpu.make_async_copy(panel.at[k], panel_ref.at[k], panel_sem.at[k]) for k in range(KP)
    ]
    doing = (send, get, weights, multiply, hop, finish)
    left = [SUBS[2 * k] + SUBS[2 * k + 1] for k in range(KP)]
    for what, which, index in STEPS:
        doing[what](which, index)
        if what == 5:
            left[which // 2] -= 1
            if left[which // 2] == 0:
                stores[which // 2].start()

    weighted = jnp.zeros((OWN, TILE), jnp.float32)
    for k in range(KP):
        weighted = weighted + weight_ref[0, k] * panel[k, 1].astype(jnp.float32)
        weighted = weighted + weight_ref[1, k] * panel[k, 0].astype(jnp.float32)
    for q in range(NP):
        piece = weighted if q == 0 else pltpu.roll(weighted, TILE - PIECE * q, 1)
        pieces[q] = piece[:, :128]
        pieces_out[q] = piece[:, :128].astype(jnp.bfloat16)
    exchange = [
        pltpu.make_async_remote_copy(
            src_ref=pieces_out.at[pole_at(by)],
            dst_ref=pieces_in.at[by - 1],
            send_sem=psend_sem.at[by - 1],
            recv_sem=precv_sem.at[by - 1],
            device_id={"pole": pole_at(by)},
            device_id_type=MESH,
        )
        for by in range(1, NP)
    ]
    for copy in exchange:
        copy.start()

    for slab in range(2 * KP):
        for j in range(NT):
            transfer(slab, j, False).wait_send()
    for store in stores:
        store.wait()
    for unit in range(NU):
        for slot in range(NS):
            for sub in range(SUBS[unit]):
                hop_copy(unit, slot, sub).wait_send()

    total = pieces[pole]
    for copy in exchange:
        copy.wait()
    for by in range(1, NP):
        total = total + pieces_in[by - 1].astype(jnp.float32)
    density_ref[...] = total[:, :PIECE]


def body(inverse, lower, mask_tiles, pole_weight):
    anywhere = pl.BlockSpec(memory_space=pl.ANY)
    vmem = pl.BlockSpec(memory_space=pltpu.VMEM)
    smem = pl.BlockSpec(memory_space=pltpu.SMEM)
    bf16, f32 = jnp.bfloat16, jnp.float32
    panel, density = pl.pallas_call(
        kernel,
        out_shape=(
            jax.ShapeDtypeStruct((KP, 2, OWN, TILE), bf16),
            jax.ShapeDtypeStruct((OWN, PIECE), f32),
        ),
        in_specs=[anywhere, anywhere, smem, smem],
        out_specs=(anywhere, vmem),
        scratch_shapes=[
            pltpu.VMEM((KP, 2, TILE, DEPTH), bf16),
            pltpu.VMEM((KP, 2, TILE, 2 * DEPTH), bf16),
            pltpu.VMEM((KP, 2, FULL, DEPTH), bf16),
            pltpu.VMEM((NU, 2, NY, HALF, TILE), f32),
            pltpu.VMEM((NU, NS, 2, HALF, TILE), bf16),
            pltpu.VMEM((NU, NS, 2, HALF, TILE), bf16),
            pltpu.VMEM((KP, 2, OWN, TILE), bf16),
            pltpu.VMEM((NP, OWN, 128), f32),
            pltpu.VMEM((NP, OWN, 128), bf16),
            pltpu.VMEM((NP - 1, OWN, 128), bf16),
            pltpu.SemaphoreType.DMA((KP,)),
            pltpu.SemaphoreType.DMA,
            pltpu.SemaphoreType.DMA((KP,)),
            pltpu.SemaphoreType.DMA((2 * KP, NT)),
            pltpu.SemaphoreType.DMA((2 * KP, NT)),
            pltpu.SemaphoreType.DMA((NU, NS, max(SUBS))),
            pltpu.SemaphoreType.DMA((NU, NS, max(SUBS))),
            pltpu.SemaphoreType.DMA((NP - 1,)),
            pltpu.SemaphoreType.DMA((NP - 1,)),
        ],
        compiler_params=pltpu.CompilerParams(
            collective_id=0, has_side_effects=True, vmem_limit_bytes=56 * 1024 * 1024
        ),
        name="panel_update",
    )(inverse, jnp.swapaxes(lower, 2, 3), mask_tiles, jnp.swapaxes(pole_weight, 0, 1))
    return jnp.swapaxes(panel, 2, 3), jnp.swapaxes(density, 0, 1)


def solution(mesh):
    return jax.shard_map(
        body,
        mesh=mesh,
        in_specs=(
            P("pole", None, "col", "row"),
            P("pole", None, "row", "col"),
            P(),
            P("pole", None),
        ),
        out_specs=(P("pole", None, "col", "row"), P(("col", "pole"), "row")),
        check_vma=False,
    )
```

```python
import jax
import jax.numpy as jnp
from jax import lax
from jax.experimental import pallas as pl
from jax.experimental.pallas import tpu as pltpu
from jax.sharding import PartitionSpec as P

MESH = pl.DeviceIdType.MESH
NX = 4
NZ = 4
NY = 8
NP = 4
KP = 3
TILE = 384
DEPTH = 768
WIDE = 32
OWN = 64
FULL = 512
PIECE = 96

ALL, LOW, HIGH = (0, 32), (0, 16), (16, 16)
TRANSFERS = (
    ((0, 0), ("z", 1), (0, -1), ALL),
    ((0, 0), ("z", -1), (0, 1), ALL),
    ((0, 0), ("x", 1), (-1, 0), ALL),
    ((0, 0), ("x", -1), (1, 0), ALL),
    ((0, -1), ("z", 1), (0, 2), LOW),
    ((0, 1), ("z", -1), (0, 2), HIGH),
    ((0, -1), ("x", 1), (-1, -1), ALL),
    ((0, -1), ("x", -1), (1, -1), ALL),
    ((0, 1), ("x", 1), (-1, 1), ALL),
    ((0, 1), ("x", -1), (1, 1), ALL),
    ((0, 2), ("x", 1), (-1, 2), ALL),
    ((0, 2), ("x", -1), (1, 2), ALL),
    ((-1, 0), ("x", 1), (2, 0), ALL),
    ((1, 2), ("x", -1), (2, 2), ALL),
    ((2, 0), ("z", 1), (2, -1), ALL),
    ((2, 0), ("z", -1), (2, 1), ALL),
)
NT = len(TRANSFERS)
NU = 2 * KP
HALF = OWN // 2
NS = 7
SUBS = (1, 1, 1, 1, 1, 2)

CHAIN = ((4, 1, ()), (3, 1, (0,)), (2, 1, (1,)), (1, 1, (2,)), (-3, -1, ()), (-2, -1, (4,)), (-1, -1, (5,)))
FAN = ((4, 2, ()), (3, 1, ()), (-3, -1, ()), (1, 1, ()), (-1, -1, ()), (2, 2, (0, 1)), (-2, -2, (2,)))
CHAIN_ENDS, FAN_ENDS = (3, 6), (3, 4, 5, 6)
LAST = NU - 1

STEPS = (
    (0, 0, 2), (0, 1, 1), (0, 0, 0), (0, 0, 3), (0, 0, 1), (0, 1, 3), (0, 1, 2), (0, 1, 0), (0, 4, 3), (0, 5, 2),
    (1, 0, 2), (0, 0, 12), (0, 2, 1), (0, 2, 3), (0, 2, 0), (0, 2, 2), (0, 3, 3), (0, 3, 2), (0, 5, 3), (2, 0, 0),
    (0, 3, 1), (0, 3, 0), (1, 0, 3), (1, 1, 2), (0, 1, 12), (1, 1, 3), (1, 1, 1), (0, 1, 9), (1, 0, 0), (1, 5, 2),
    (0, 0, 7), (0, 1, 8), (1, 4, 3), (1, 0, 12), (0, 0, 15), (0, 0, 14), (0, 0, 6), (1, 2, 3), (1, 0, 1), (0, 0, 9),
    (1, 1, 0), (1, 2, 2), (0, 1, 5), (0, 1, 7), (0, 0, 8), (0, 1, 4), (1, 3, 3), (1, 3, 2), (0, 0, 5), (0, 2, 12),
    (0, 0, 4), (1, 5, 3), (1, 2, 1), (0, 2, 9), (1, 2, 0), (1, 1, 12), (0, 1, 15), (0, 2, 7), (0, 1, 14), (0, 1, 6),
    (1, 1, 9), (1, 1, 8), (0, 2, 8), (1, 0, 7), (1, 3, 1), (0, 3, 9), (1, 3, 0), (1, 0, 6), (0, 3, 8), (0, 2, 5),
    (0, 2, 4), (0, 3, 7), (1, 0, 9), (1, 0, 8), (0, 3, 5), (0, 3, 4), (0, 3, 12), (1, 1, 7), (1, 0, 15), (1, 0, 14),
    (1, 2, 12), (0, 2, 15), (0, 2, 14), (0, 2, 6), (1, 2, 9), (1, 1, 5), (1, 1, 4), (0, 1, 11), (1, 1, 6),
    (0, 1, 10), (1, 2, 7), (1, 0, 5), (1, 0, 4), (0, 0, 11), (1, 2, 8), (0, 0, 10), (0, 5, 1), (0, 4, 0), (1, 3, 9),
    (1, 3, 8), (0, 4, 2), (1, 3, 7), (1, 1, 15), (1, 1, 14), (3, 0, 0), (0, 5, 12), (3, 0, 1), (0, 4, 1), (0, 5, 0),
    (4, 0, 0), (0, 3, 6), (4, 0, 32), (1, 3, 12), (1, 1, 11), (0, 1, 13), (1, 2, 5), (1, 2, 4), (0, 2, 11),
    (1, 2, 6), (1, 0, 11), (0, 0, 13), (1, 3, 5), (1, 3, 4), (1, 1, 10), (0, 3, 15), (0, 3, 11), (0, 3, 14),
    (0, 2, 10), (1, 0, 10), (0, 3, 10), (1, 2, 15), (1, 2, 14), (4, 0, 8), (1, 4, 2), (0, 4, 12), (4, 0, 40),
    (1, 1, 13), (1, 5, 12), (0, 5, 15), (0, 5, 14), (1, 2, 11), (0, 2, 13), (1, 5, 1), (0, 5, 8), (0, 5, 9),
    (1, 4, 0), (0, 4, 7), (1, 3, 6), (0, 4, 4), (0, 5, 5), (0, 4, 6), (1, 0, 13), (3, 1, 0), (3, 1, 1), (4, 1, 0),
    (4, 1, 32), (2, 1, 0), (4, 0, 16), (4, 0, 48), (1, 2, 10), (1, 3, 11), (0, 3, 13), (1, 4, 1), (0, 4, 8),
    (0, 4, 5), (0, 4, 9), (1, 5, 0), (0, 5, 4), (0, 5, 7), (0, 5, 6), (1, 3, 10), (1, 2, 13), (1, 4, 12),
    (0, 4, 15), (0, 4, 14), (1, 3, 15), (1, 3, 14), (3, 2, 0), (3, 2, 1), (4, 2, 0), (4, 2, 32), (1, 5, 9),
    (1, 5, 8), (1, 4, 7), (4, 1, 8), (4, 1, 40), (1, 4, 6), (1, 5, 15), (1, 5, 14), (1, 3, 13), (3, 3, 0),
    (4, 0, 24), (3, 3, 1), (4, 3, 0), (4, 3, 32), (2, 2, 0), (1, 4, 8), (1, 5, 5), (1, 4, 4), (1, 4, 9), (1, 5, 6),
    (1, 4, 5), (0, 4, 10), (0, 4, 11), (1, 5, 4), (0, 5, 11), (0, 5, 10), (1, 5, 7), (4, 2, 8), (4, 2, 40),
    (4, 1, 48), (4, 1, 16), (1, 4, 15), (1, 4, 14), (3, 4, 0), (3, 4, 1), (4, 4, 0), (4, 4, 32), (4, 3, 8),
    (5, 0, 0), (4, 3, 40), (1, 4, 10), (1, 4, 11), (0, 4, 13), (4, 2, 48), (4, 2, 16), (1, 5, 10), (1, 5, 11),
    (0, 5, 13), (4, 1, 24), (4, 4, 8), (4, 4, 40), (1, 4, 13), (4, 3, 48), (4, 3, 16), (1, 5, 13), (3, 5, 0),
    (4, 2, 24), (4, 5, 0), (4, 5, 8), (4, 5, 16), (4, 5, 24), (4, 5, 32), (3, 5, 1), (4, 5, 1), (4, 5, 9),
    (4, 5, 17), (4, 5, 25), (4, 4, 16), (4, 5, 33), (5, 1, 0), (4, 4, 48), (4, 3, 24), (4, 5, 48), (5, 2, 0),
    (4, 5, 40), (4, 5, 41), (4, 5, 49), (4, 4, 24), (5, 3, 0), (5, 5, 0), (5, 5, 1), (5, 4, 0),
)


def kernel(
    inverse_ref, lower_ref, mask_ref, weight_ref, panel_ref, density_ref,
    block, factor, gathered, product, outgoing, incoming, panel, pieces, pieces_out, pieces_in,
    block_sem, own_sem, panel_sem, send_sem, recv_sem, rsend_sem, rrecv_sem, psend_sem, precv_sem,
):
    pole = lax.axis_index("pole")
    row = lax.axis_index("row")
    col = lax.axis_index("col")
    x, z = col // NZ, col % NZ

    def place(dx, dz):
        return lax.rem(x + NX + dx, NX) * NZ + lax.rem(z + NZ + dz, NZ)

    def along(step):
        axis, by = step
        return place(by, 0) if axis == "x" else place(0, by)

    def row_at(by):
        return lax.rem(row + NY + by, NY)

    def pole_at(by):
        return lax.rem(pole + by, NP)

    loads = [
        pltpu.make_async_copy(inverse_ref.at[k], block.at[k], block_sem.at[k]) for k in range(KP)
    ]
    first_own = pl.multiple_of(place(0, 0) * WIDE, WIDE)
    own = pltpu.make_async_copy(lower_ref, gathered.at[:, :, pl.ds(first_own, WIDE), :], own_sem)
    own.start()
    for load in loads:
        load.start()

    barrier = pltpu.get_barrier_semaphore()
    for step in (("x", 1), ("x", -1), ("z", 1), ("z", -1)):
        pl.semaphore_signal(barrier, inc=1, device_id={"col": along(step)}, device_id_type=MESH)
    for by in (1, -1, 2, -2):
        pl.semaphore_signal(barrier, inc=1, device_id={"row": row_at(by)}, device_id_type=MESH)
    for by in (1, 2, 3):
        pl.semaphore_signal(barrier, inc=1, device_id={"pole": pole_at(by)}, device_id_type=MESH)
    pl.semaphore_wait(barrier, 11)

    def spot(slab, chunk, rows):
        first = pl.multiple_of(place(*chunk) * WIDE + rows[0], 16)
        return gathered.at[slab // 2, slab % 2, pl.ds(first, rows[1]), :]

    def transfer(slab, j, receiving):
        sent, step, got, rows = TRANSFERS[j]
        where = spot(slab, got if receiving else sent, rows)
        source = where
        if not receiving and sent == (0, 0):
            source = lower_ref.at[slab // 2, slab % 2]
        return pltpu.make_async_remote_copy(
            src_ref=source,
            dst_ref=where,
            send_sem=send_sem.at[slab, j],
            recv_sem=recv_sem.at[slab, j],
            device_id={"col": along(step)},
            device_id_type=MESH,
        )

    def send(slab, j):
        transfer(slab, j, False).start()

    def get(slab, j):
        transfer(slab, j, True).wait_recv()

    def weights(k, _):
        loads[k].wait()
        if k == 0:
            own.wait()
        left = mask_ref[col, 2 * row].astype(jnp.float32)
        right = mask_ref[col, 2 * row + 1].astype(jnp.float32)
        lane = lax.broadcasted_iota(jnp.int32, (1, DEPTH), 1)
        keep = jnp.where(lane < TILE, left, right)

        def some(i, carry):
            first = pl.multiple_of(i * 64, 64)
            re = block[k, 0, pl.ds(first, 64), :].astype(jnp.float32) * keep
            im = block[k, 1, pl.ds(first, 64), :].astype(jnp.float32) * keep
            minus_re = (-re).astype(jnp.bfloat16)
            factor[k, 0, pl.ds(first, 64), :DEPTH] = minus_re
            factor[k, 0, pl.ds(first, 64), DEPTH:] = im.astype(jnp.bfloat16)
            factor[k, 1, pl.ds(first, 64), :DEPTH] = (-im).astype(jnp.bfloat16)
            factor[k, 1, pl.ds(first, 64), DEPTH:] = minus_re
            return carry

        lax.fori_loop(0, TILE // 64, some, 0)

    def spread(unit, owner):
        odd = lax.rem(z + 1 + unit % 2, 2)
        return pl.ds(pl.multiple_of(row_at(owner) * OWN + odd * HALF, HALF), HALF)

    def multiply(unit, part):
        k = unit // 2
        lines = []
        for owner in range(NY):
            rows = spread(unit, owner)
            lines.append(jnp.concatenate([gathered[k, 0, rows, :], gathered[k, 1, rows, :]], axis=1))
        value = lax.dot_general(
            jnp.concatenate(lines, axis=0),
            factor[k, part],
            (((1,), (1,)), ((), ())),
            preferred_element_type=jnp.float32,
        )
        product[unit, part] = value.reshape(NY, HALF, TILE)

    def way(unit, slot, sub):
        turn = 1 if (sub if unit == LAST else unit) % 2 == 0 else -1
        owner, step, needs = (FAN if unit == LAST else CHAIN)[slot]
        return turn * owner % 8, turn * step, needs

    def parts_of(unit, sub):
        return slice(None) if SUBS[unit] == 1 else slice(sub, sub + 1)

    def hop_copy(unit, slot, sub):
        parts = pl.ds(0, 2) if SUBS[unit] == 1 else pl.ds(sub, 1)
        return pltpu.make_async_remote_copy(
            src_ref=outgoing.at[unit, slot, parts],
            dst_ref=incoming.at[unit, slot, parts],
            send_sem=rsend_sem.at[unit, slot, sub],
            recv_sem=rrecv_sem.at[unit, slot, sub],
            device_id={"row": row_at(way(unit, slot, sub)[1])},
            device_id_type=MESH,
        )

    def summed(unit, owner, slots, sub):
        parts = parts_of(unit, sub)
        value = product[unit, parts, owner]
        for slot in slots:
            hop_copy(unit, slot, sub).wait_recv()
            value = value + incoming[unit, slot, parts].astype(jnp.float32)
        return value.astype(jnp.bfloat16)

    def hop(unit, index):
        slot, sub = index // 8, index % 8
        owner, _, needs = way(unit, slot, sub)
        outgoing[unit, slot, parts_of(unit, sub)] = summed(unit, owner, needs, sub)
        hop_copy(unit, slot, sub).start()

    def finish(unit, sub):
        odd = lax.rem(z + 1 + unit % 2, 2)
        rows = pl.ds(pl.multiple_of(odd * HALF, HALF), HALF)
        ends = FAN_ENDS if unit == LAST else CHAIN_ENDS
        panel[unit // 2, parts_of(unit, sub), rows, :] = summed(unit, 0, ends, sub)

    stores = [
        pltpu.make_async_copy(panel.at[k], panel_ref.at[k], panel_sem.at[k]) for k in range(KP)
    ]
    doing = (send, get, weights, multiply, hop, finish)
    left = [SUBS[2 * k] + SUBS[2 * k + 1] for k in range(KP)]
    for what, which, index in STEPS:
        doing[what](which, index)
        if what == 5:
            left[which // 2] -= 1
            if left[which // 2] == 0:
                stores[which // 2].start()

    weighted = jnp.zeros((OWN, TILE), jnp.float32)
    for k in range(KP):
        weighted = weighted + weight_ref[0, k] * panel[k, 1].astype(jnp.float32)
        weighted = weighted + weight_ref[1, k] * panel[k, 0].astype(jnp.float32)
    for q in range(NP):
        piece = weighted if q == 0 else pltpu.roll(weighted, TILE - PIECE * q, 1)
        pieces[q] = piece[:, :128]
        pieces_out[q] = piece[:, :128].astype(jnp.bfloat16)
    exchange = [
        pltpu.make_async_remote_copy(
            src_ref=pieces_out.at[pole_at(by)],
            dst_ref=pieces_in.at[by - 1],
            send_sem=psend_sem.at[by - 1],
            recv_sem=precv_sem.at[by - 1],
            device_id={"pole": pole_at(by)},
            device_id_type=MESH,
        )
        for by in range(1, NP)
    ]
    for copy in exchange:
        copy.start()

    for slab in range(2 * KP):
        for j in range(NT):
            transfer(slab, j, False).wait_send()
    for store in stores:
        store.wait()
    for unit in range(NU):
        for slot in range(NS):
            for sub in range(SUBS[unit]):
                hop_copy(unit, slot, sub).wait_send()

    total = pieces[pole]
    for copy in exchange:
        copy.wait()
    for by in range(1, NP):
        total = total + pieces_in[by - 1].astype(jnp.float32)
    density_ref[...] = total[:, :PIECE]


def hand_over(panel_ref, density_ref, panel_out, density_out, sem):
    copies = [
        pltpu.make_async_copy(panel_ref, panel_out, sem.at[0]),
        pltpu.make_async_copy(density_ref, density_out, sem.at[1]),
    ]
    for copy in copies:
        copy.start()
    for copy in copies:
        copy.wait()


def body(inverse, lower, mask_tiles, pole_weight):
    anywhere = pl.BlockSpec(memory_space=pl.ANY)
    vmem = pl.BlockSpec(memory_space=pltpu.VMEM)
    smem = pl.BlockSpec(memory_space=pltpu.SMEM)
    bf16, f32 = jnp.bfloat16, jnp.float32
    arrays = pl.pallas_call(
        kernel,
        out_shape=(
            jax.ShapeDtypeStruct((KP, 2, OWN, TILE), bf16),
            jax.ShapeDtypeStruct((OWN, PIECE), f32),
        ),
        in_specs=[anywhere, anywhere, smem, smem],
        out_specs=(anywhere, vmem),
        scratch_shapes=[
            pltpu.VMEM((KP, 2, TILE, DEPTH), bf16),
            pltpu.VMEM((KP, 2, TILE, 2 * DEPTH), bf16),
            pltpu.VMEM((KP, 2, FULL, DEPTH), bf16),
            pltpu.VMEM((NU, 2, NY, HALF, TILE), f32),
            pltpu.VMEM((NU, NS, 2, HALF, TILE), bf16),
            pltpu.VMEM((NU, NS, 2, HALF, TILE), bf16),
            pltpu.VMEM((KP, 2, OWN, TILE), bf16),
            pltpu.VMEM((NP, OWN, 128), f32),
            pltpu.VMEM((NP, OWN, 128), bf16),
            pltpu.VMEM((NP - 1, OWN, 128), bf16),
            pltpu.SemaphoreType.DMA((KP,)),
            pltpu.SemaphoreType.DMA,
            pltpu.SemaphoreType.DMA((KP,)),
            pltpu.SemaphoreType.DMA((2 * KP, NT)),
            pltpu.SemaphoreType.DMA((2 * KP, NT)),
            pltpu.SemaphoreType.DMA((NU, NS, max(SUBS))),
            pltpu.SemaphoreType.DMA((NU, NS, max(SUBS))),
            pltpu.SemaphoreType.DMA((NP - 1,)),
            pltpu.SemaphoreType.DMA((NP - 1,)),
        ],
        compiler_params=pltpu.CompilerParams(
            collective_id=0, has_side_effects=True, vmem_limit_bytes=56 * 1024 * 1024
        ),
        name="panel_update",
    )(inverse, jnp.swapaxes(lower, 2, 3), mask_tiles, jnp.swapaxes(pole_weight, 0, 1))
    panel, density = pl.pallas_call(
        hand_over,
        out_shape=tuple(jax.ShapeDtypeStruct(array.shape, array.dtype) for array in arrays),
        in_specs=[vmem, vmem],
        out_specs=(anywhere, anywhere),
        scratch_shapes=[pltpu.SemaphoreType.DMA((2,))],
        name="hand_over",
    )(*arrays)
    return jnp.swapaxes(panel, 2, 3), jnp.swapaxes(density, 0, 1)


def solution(mesh):
    return jax.shard_map(
        body,
        mesh=mesh,
        in_specs=(
            P("pole", None, "col", "row"),
            P("pole", None, "row", "col"),
            P(),
            P("pole", None),
        ),
        out_specs=(P("pole", None, "col", "row"), P(("col", "pole"), "row")),
        check_vma=False,
    )
```

```python
import jax
import jax.numpy as jnp
from jax import lax
from jax.experimental import pallas as pl
from jax.experimental.pallas import tpu as pltpu
from jax.sharding import PartitionSpec as P

MESH = pl.DeviceIdType.MESH
NX = 4
NZ = 4
NY = 8
NP = 4
KP = 3
TILE = 384
DEPTH = 768
WIDE = 32
OWN = 64
FULL = 512
PIECE = 96

ALL, LOW, HIGH = (0, 32), (0, 16), (16, 16)
TRANSFERS = (
    ((0, 0), ("z", 1), (0, -1), ALL),
    ((0, 0), ("z", -1), (0, 1), ALL),
    ((0, 0), ("x", 1), (-1, 0), ALL),
    ((0, 0), ("x", -1), (1, 0), ALL),
    ((0, -1), ("z", 1), (0, 2), LOW),
    ((0, 1), ("z", -1), (0, 2), HIGH),
    ((0, -1), ("x", 1), (-1, -1), ALL),
    ((0, -1), ("x", -1), (1, -1), ALL),
    ((0, 1), ("x", 1), (-1, 1), ALL),
    ((0, 1), ("x", -1), (1, 1), ALL),
    ((0, 2), ("x", 1), (-1, 2), ALL),
    ((0, 2), ("x", -1), (1, 2), ALL),
    ((-1, 0), ("x", 1), (2, 0), ALL),
    ((1, 2), ("x", -1), (2, 2), ALL),
    ((2, 0), ("z", 1), (2, -1), ALL),
    ((2, 0), ("z", -1), (2, 1), ALL),
)
NT = len(TRANSFERS)
NU = 2 * KP
HALF = OWN // 2
NS = 7
SUBS = (1, 1, 1, 1, 1, 2)

CHAIN = ((4, 1, ()), (3, 1, (0,)), (2, 1, (1,)), (1, 1, (2,)), (-3, -1, ()), (-2, -1, (4,)), (-1, -1, (5,)))
FAN = ((4, 2, ()), (3, 1, ()), (-3, -1, ()), (1, 1, ()), (-1, -1, ()), (2, 2, (0, 1)), (-2, -2, (2,)))
CHAIN_ENDS, FAN_ENDS = (3, 6), (3, 4, 5, 6)
LAST = NU - 1

STEPS = (
    (0, 0, 2), (0, 1, 1), (0, 0, 0), (0, 0, 3), (0, 0, 1), (0, 1, 3), (0, 1, 2), (0, 1, 0), (0, 4, 3), (0, 5, 2),
    (1, 0, 2), (0, 0, 12), (0, 2, 1), (0, 2, 3), (0, 2, 0), (0, 2, 2), (0, 3, 3), (0, 3, 2), (0, 5, 3), (2, 0, 0),
    (0, 3, 1), (0, 3, 0), (1, 0, 3), (1, 1, 2), (0, 1, 12), (1, 1, 3), (1, 1, 1), (0, 1, 9), (1, 0, 0), (1, 5, 2),
    (0, 0, 7), (0, 1, 8), (1, 4, 3), (1, 0, 12), (0, 0, 15), (0, 0, 14), (0, 0, 6), (1, 2, 3), (1, 0, 1), (0, 0, 9),
    (1, 1, 0), (1, 2, 2), (0, 1, 5), (0, 1, 7), (0, 0, 8), (0, 1, 4), (1, 3, 3), (1, 3, 2), (0, 0, 5), (0, 2, 12),
    (0, 0, 4), (1, 5, 3), (1, 2, 1), (0, 2, 9), (1, 2, 0), (1, 1, 12), (0, 1, 15), (0, 2, 7), (0, 1, 14), (0, 1, 6),
    (1, 1, 9), (1, 1, 8), (0, 2, 8), (1, 0, 7), (1, 3, 1), (0, 3, 9), (1, 3, 0), (1, 0, 6), (0, 3, 8), (0, 2, 5),
    (0, 2, 4), (0, 3, 7), (1, 0, 9), (1, 0, 8), (0, 3, 5), (0, 3, 4), (0, 3, 12), (1, 1, 7), (1, 0, 15), (1, 0, 14),
    (1, 2, 12), (0, 2, 15), (0, 2, 14), (0, 2, 6), (1, 2, 9), (1, 1, 5), (1, 1, 4), (0, 1, 11), (1, 1, 6),
    (0, 1, 10), (1, 2, 7), (1, 0, 5), (1, 0, 4), (0, 0, 11), (1, 2, 8), (0, 0, 10), (0, 5, 1), (0, 4, 0), (1, 3, 9),
    (1, 3, 8), (0, 4, 2), (1, 3, 7), (1, 1, 15), (1, 1, 14), (3, 0, 0), (0, 5, 12), (3, 0, 1), (0, 4, 1), (0, 5, 0),
    (4, 0, 0), (0, 3, 6), (4, 0, 32), (1, 3, 12), (1, 1, 11), (0, 1, 13), (1, 2, 5), (1, 2, 4), (0, 2, 11),
    (1, 2, 6), (1, 0, 11), (0, 0, 13), (1, 3, 5), (1, 3, 4), (1, 1, 10), (0, 3, 15), (0, 3, 11), (0, 3, 14),
    (0, 2, 10), (1, 0, 10), (0, 3, 10), (1, 2, 15), (1, 2, 14), (4, 0, 8), (1, 4, 2), (0, 4, 12), (4, 0, 40),
    (1, 1, 13), (1, 5, 12), (0, 5, 15), (0, 5, 14), (1, 2, 11), (0, 2, 13), (1, 5, 1), (0, 5, 8), (0, 5, 9),
    (1, 4, 0), (0, 4, 7), (1, 3, 6), (0, 4, 4), (0, 5, 5), (0, 4, 6), (1, 0, 13), (3, 1, 0), (3, 1, 1), (4, 1, 0),
    (4, 1, 32), (2, 1, 0), (4, 0, 16), (4, 0, 48), (1, 2, 10), (1, 3, 11), (0, 3, 13), (1, 4, 1), (0, 4, 8),
    (0, 4, 5), (0, 4, 9), (1, 5, 0), (0, 5, 4), (0, 5, 7), (0, 5, 6), (1, 3, 10), (1, 2, 13), (1, 4, 12),
    (0, 4, 15), (0, 4, 14), (1, 3, 15), (1, 3, 14), (3, 2, 0), (3, 2, 1), (4, 2, 0), (4, 2, 32), (1, 5, 9),
    (1, 5, 8), (1, 4, 7), (4, 1, 8), (4, 1, 40), (1, 4, 6), (1, 5, 15), (1, 5, 14), (1, 3, 13), (3, 3, 0),
    (4, 0, 24), (3, 3, 1), (4, 3, 0), (4, 3, 32), (2, 2, 0), (1, 4, 8), (1, 5, 5), (1, 4, 4), (1, 4, 9), (1, 5, 6),
    (1, 4, 5), (0, 4, 10), (0, 4, 11), (1, 5, 4), (0, 5, 11), (0, 5, 10), (1, 5, 7), (4, 2, 8), (4, 2, 40),
    (4, 1, 48), (4, 1, 16), (1, 4, 15), (1, 4, 14), (3, 4, 0), (3, 4, 1), (4, 4, 0), (4, 4, 32), (4, 3, 8),
    (5, 0, 0), (4, 3, 40), (1, 4, 10), (1, 4, 11), (0, 4, 13), (4, 2, 48), (4, 2, 16), (1, 5, 10), (1, 5, 11),
    (0, 5, 13), (4, 1, 24), (4, 4, 8), (4, 4, 40), (1, 4, 13), (4, 3, 48), (4, 3, 16), (1, 5, 13), (3, 5, 0),
    (4, 2, 24), (4, 5, 0), (4, 5, 8), (4, 5, 16), (4, 5, 24), (4, 5, 32), (3, 5, 1), (4, 5, 1), (4, 5, 9),
    (4, 5, 17), (4, 5, 25), (4, 4, 16), (4, 5, 33), (5, 1, 0), (4, 4, 48), (4, 3, 24), (4, 5, 48), (5, 2, 0),
    (4, 5, 40), (4, 5, 41), (4, 5, 49), (4, 4, 24), (5, 3, 0), (5, 5, 0), (5, 5, 1), (5, 4, 0),
)


def kernel(
    inverse_ref, lower_ref, mask_ref, weight_ref, panel_ref, density_ref,
    block, factor, gathered, product, outgoing, incoming, panel, pieces, pieces_out, pieces_in,
    block_sem, own_sem, panel_sem, send_sem, recv_sem, rsend_sem, rrecv_sem, psend_sem, precv_sem,
):
    pole = lax.axis_index("pole")
    row = lax.axis_index("row")
    col = lax.axis_index("col")
    x, z = col // NZ, col % NZ

    def place(dx, dz):
        return lax.rem(x + NX + dx, NX) * NZ + lax.rem(z + NZ + dz, NZ)

    def along(step):
        axis, by = step
        return place(by, 0) if axis == "x" else place(0, by)

    def row_at(by):
        return lax.rem(row + NY + by, NY)

    def pole_at(by):
        return lax.rem(pole + by, NP)

    loads = [
        pltpu.make_async_copy(inverse_ref.at[k], block.at[k], block_sem.at[k]) for k in range(KP)
    ]
    first_own = pl.multiple_of(place(0, 0) * WIDE, WIDE)
    own = pltpu.make_async_copy(lower_ref, gathered.at[:, :, pl.ds(first_own, WIDE), :], own_sem)

    barrier = pltpu.get_barrier_semaphore()
    for step in (("x", 1), ("x", -1), ("z", 1), ("z", -1)):
        pl.semaphore_signal(barrier, inc=1, device_id={"col": along(step)}, device_id_type=MESH)
    for by in (1, -1, 2, -2):
        pl.semaphore_signal(barrier, inc=1, device_id={"row": row_at(by)}, device_id_type=MESH)
    for by in (1, 2, 3):
        pl.semaphore_signal(barrier, inc=1, device_id={"pole": pole_at(by)}, device_id_type=MESH)
    own.start()
    for load in loads:
        load.start()
    pl.semaphore_wait(barrier, 11)

    def spot(slab, chunk, rows):
        first = pl.multiple_of(place(*chunk) * WIDE + rows[0], 16)
        return gathered.at[slab // 2, slab % 2, pl.ds(first, rows[1]), :]

    def transfer(slab, j, receiving):
        sent, step, got, rows = TRANSFERS[j]
        where = spot(slab, got if receiving else sent, rows)
        source = where
        if not receiving and sent == (0, 0):
            source = lower_ref.at[slab // 2, slab % 2]
        return pltpu.make_async_remote_copy(
            src_ref=source,
            dst_ref=where,
            send_sem=send_sem.at[slab, j],
            recv_sem=recv_sem.at[slab, j],
            device_id={"col": along(step)},
            device_id_type=MESH,
        )

    def send(slab, j):
        transfer(slab, j, False).start()

    def get(slab, j):
        transfer(slab, j, True).wait_recv()

    def weights(k, _):
        loads[k].wait()
        if k == 0:
            own.wait()
        left = mask_ref[col, 2 * row].astype(jnp.float32)
        right = mask_ref[col, 2 * row + 1].astype(jnp.float32)
        lane = lax.broadcasted_iota(jnp.int32, (1, DEPTH), 1)
        keep = jnp.where(lane < TILE, left, right)

        def some(i, carry):
            first = pl.multiple_of(i * 64, 64)
            re = block[k, 0, pl.ds(first, 64), :].astype(jnp.float32) * keep
            im = block[k, 1, pl.ds(first, 64), :].astype(jnp.float32) * keep
            minus_re = (-re).astype(jnp.bfloat16)
            factor[k, 0, pl.ds(first, 64), :DEPTH] = minus_re
            factor[k, 0, pl.ds(first, 64), DEPTH:] = im.astype(jnp.bfloat16)
            factor[k, 1, pl.ds(first, 64), :DEPTH] = (-im).astype(jnp.bfloat16)
            factor[k, 1, pl.ds(first, 64), DEPTH:] = minus_re
            return carry

        lax.fori_loop(0, TILE // 64, some, 0)

    def spread(unit, owner):
        odd = lax.rem(z + 1 + unit % 2, 2)
        return pl.ds(pl.multiple_of(row_at(owner) * OWN + odd * HALF, HALF), HALF)

    def multiply(unit, part):
        k = unit // 2
        lines = []
        for owner in range(NY):
            rows = spread(unit, owner)
            lines.append(jnp.concatenate([gathered[k, 0, rows, :], gathered[k, 1, rows, :]], axis=1))
        value = lax.dot_general(
            jnp.concatenate(lines, axis=0),
            factor[k, part],
            (((1,), (1,)), ((), ())),
            preferred_element_type=jnp.float32,
        )
        product[unit, part] = value.reshape(NY, HALF, TILE)

    def way(unit, slot, sub):
        turn = 1 if (sub if unit == LAST else unit) % 2 == 0 else -1
        owner, step, needs = (FAN if unit == LAST else CHAIN)[slot]
        return turn * owner % 8, turn * step, needs

    def parts_of(unit, sub):
        return slice(None) if SUBS[unit] == 1 else slice(sub, sub + 1)

    def hop_copy(unit, slot, sub):
        parts = pl.ds(0, 2) if SUBS[unit] == 1 else pl.ds(sub, 1)
        return pltpu.make_async_remote_copy(
            src_ref=outgoing.at[unit, slot, parts],
            dst_ref=incoming.at[unit, slot, parts],
            send_sem=rsend_sem.at[unit, slot, sub],
            recv_sem=rrecv_sem.at[unit, slot, sub],
            device_id={"row": row_at(way(unit, slot, sub)[1])},
            device_id_type=MESH,
        )

    def summed(unit, owner, slots, sub):
        parts = parts_of(unit, sub)
        value = product[unit, parts, owner]
        for slot in slots:
            hop_copy(unit, slot, sub).wait_recv()
            value = value + incoming[unit, slot, parts].astype(jnp.float32)
        return value.astype(jnp.bfloat16)

    def hop(unit, index):
        slot, sub = index // 8, index % 8
        owner, _, needs = way(unit, slot, sub)
        outgoing[unit, slot, parts_of(unit, sub)] = summed(unit, owner, needs, sub)
        hop_copy(unit, slot, sub).start()

    def finish(unit, sub):
        odd = lax.rem(z + 1 + unit % 2, 2)
        rows = pl.ds(pl.multiple_of(odd * HALF, HALF), HALF)
        ends = FAN_ENDS if unit == LAST else CHAIN_ENDS
        panel[unit // 2, parts_of(unit, sub), rows, :] = summed(unit, 0, ends, sub)

    stores = [
        pltpu.make_async_copy(panel.at[k], panel_ref.at[k], panel_sem.at[k]) for k in range(KP)
    ]
    doing = (send, get, weights, multiply, hop, finish)
    left = [SUBS[2 * k] + SUBS[2 * k + 1] for k in range(KP)]
    for what, which, index in STEPS:
        doing[what](which, index)
        if what == 5:
            left[which // 2] -= 1
            if left[which // 2] == 0:
                stores[which // 2].start()

    weighted = jnp.zeros((OWN, TILE), jnp.float32)
    for k in range(KP):
        weighted = weighted + weight_ref[0, k] * panel[k, 1].astype(jnp.float32)
        weighted = weighted + weight_ref[1, k] * panel[k, 0].astype(jnp.float32)
    for q in range(NP):
        piece = weighted if q == 0 else pltpu.roll(weighted, TILE - PIECE * q, 1)
        pieces[q] = piece[:, :128]
        pieces_out[q] = piece[:, :128].astype(jnp.bfloat16)
    exchange = [
        pltpu.make_async_remote_copy(
            src_ref=pieces_out.at[pole_at(by)],
            dst_ref=pieces_in.at[by - 1],
            send_sem=psend_sem.at[by - 1],
            recv_sem=precv_sem.at[by - 1],
            device_id={"pole": pole_at(by)},
            device_id_type=MESH,
        )
        for by in range(1, NP)
    ]
    for copy in exchange:
        copy.start()

    for slab in range(2 * KP):
        for j in range(NT):
            transfer(slab, j, False).wait_send()
    for store in stores:
        store.wait()
    for unit in range(NU):
        for slot in range(NS):
            for sub in range(SUBS[unit]):
                hop_copy(unit, slot, sub).wait_send()

    total = pieces[pole]
    for copy in exchange:
        copy.wait()
    for by in range(1, NP):
        total = total + pieces_in[by - 1].astype(jnp.float32)
    density_ref[...] = total[:, :PIECE]


def hand_over(panel_ref, density_ref, panel_out, density_out, sem):
    copies = [
        pltpu.make_async_copy(panel_ref, panel_out, sem.at[0]),
        pltpu.make_async_copy(density_ref, density_out, sem.at[1]),
    ]
    for copy in copies:
        copy.start()
    for copy in copies:
        copy.wait()


def body(inverse, lower, mask_tiles, pole_weight):
    anywhere = pl.BlockSpec(memory_space=pl.ANY)
    vmem = pl.BlockSpec(memory_space=pltpu.VMEM)
    smem = pl.BlockSpec(memory_space=pltpu.SMEM)
    bf16, f32 = jnp.bfloat16, jnp.float32
    arrays = pl.pallas_call(
        kernel,
        out_shape=(
            jax.ShapeDtypeStruct((KP, 2, OWN, TILE), bf16),
            jax.ShapeDtypeStruct((OWN, PIECE), f32),
        ),
        in_specs=[anywhere, anywhere, smem, smem],
        out_specs=(anywhere, vmem),
        scratch_shapes=[
            pltpu.VMEM((KP, 2, TILE, DEPTH), bf16),
            pltpu.VMEM((KP, 2, TILE, 2 * DEPTH), bf16),
            pltpu.VMEM((KP, 2, FULL, DEPTH), bf16),
            pltpu.VMEM((NU, 2, NY, HALF, TILE), f32),
            pltpu.VMEM((NU, NS, 2, HALF, TILE), bf16),
            pltpu.VMEM((NU, NS, 2, HALF, TILE), bf16),
            pltpu.VMEM((KP, 2, OWN, TILE), bf16),
            pltpu.VMEM((NP, OWN, 128), f32),
            pltpu.VMEM((NP, OWN, 128), bf16),
            pltpu.VMEM((NP - 1, OWN, 128), bf16),
            pltpu.SemaphoreType.DMA((KP,)),
            pltpu.SemaphoreType.DMA,
            pltpu.SemaphoreType.DMA((KP,)),
            pltpu.SemaphoreType.DMA((2 * KP, NT)),
            pltpu.SemaphoreType.DMA((2 * KP, NT)),
            pltpu.SemaphoreType.DMA((NU, NS, max(SUBS))),
            pltpu.SemaphoreType.DMA((NU, NS, max(SUBS))),
            pltpu.SemaphoreType.DMA((NP - 1,)),
            pltpu.SemaphoreType.DMA((NP - 1,)),
        ],
        compiler_params=pltpu.CompilerParams(
            collective_id=0, has_side_effects=True, vmem_limit_bytes=56 * 1024 * 1024
        ),
        name="panel_update",
    )(inverse, jnp.swapaxes(lower, 2, 3), mask_tiles, jnp.swapaxes(pole_weight, 0, 1))
    panel, density = pl.pallas_call(
        hand_over,
        out_shape=tuple(jax.ShapeDtypeStruct(array.shape, array.dtype) for array in arrays),
        in_specs=[vmem, vmem],
        out_specs=(anywhere, anywhere),
        scratch_shapes=[pltpu.SemaphoreType.DMA((2,))],
        name="hand_over",
    )(*arrays)
    return jnp.swapaxes(panel, 2, 3), jnp.swapaxes(density, 0, 1)


def solution(mesh):
    return jax.shard_map(
        body,
        mesh=mesh,
        in_specs=(
            P("pole", None, "col", "row"),
            P("pole", None, "row", "col"),
            P(),
            P("pole", None),
        ),
        out_specs=(P("pole", None, "col", "row"), P(("col", "pole"), "row")),
        check_vma=False,
    )
```
